256 devices in a mesh: row: 32 (over x, y, core), col: 8 (over z).
Axes of the slice: x: 4, y: 4, z: 8, core: 2. Of those that a mesh axis runs over, the one named last changes fastest.
Arguments:
- block_values: bfloat16 [32, 8, 192, 128, 128], P('row', 'col'), may hold values from -0.0625 to 0.0625
- block_rows: int32 [32, 8, 192], P('row', 'col'), may hold values from 0 to 4095, as said below
- block_cols: int32 [32, 8, 192], P('row', 'col'), may hold values from 0 to 4095, as said below
- block_counts: int32 [32, 8], P('row', 'col'), may hold values from 48 to 192, as said below
- precond: float32 [8, 512, 128, 128], P('col', 'row')
- right_side: float32 [8, 512, 32, 128], P('col', 'row'), may hold values from -6 to 6
Outputs:
- solution: float32 [8, 512, 32, 128], P('col', 'row')
The draws below stay inside these ranges and needn't reach their ends.
Inputs may be any that keep to these rules, and one draw needn't show every extreme that they name: `block_rows`: the block rows of device (r, c) lie in [c * 512, (c + 1) * 512); positions may repeat; for each j, at most 9 of a device's 192 slots have (row mod 512) // 16 == j, and in every index of col some j has exactly 9 such slots on every device. `block_cols`: every block column q of device (r, c) has (q mod 512) // 16 == r; positions may repeat. `block_counts`: slots at or past a device's count are unused; some device uses all 192 slots.
All inputs are finite; a program needn't handle non-finite values.
Results may differ from the reference program's by a relative error of at most 0.00073.
Values may be sent and summed in bfloat16 or wider, within the bound.
A program may use at most 64 MiB of HBM per device.

```python
import jax
import jax.numpy as jnp
from jax import lax

BS = 128
OWN_DEV = 16
BLK_DEV = 192
RHS = 32
ITERS = 3
RGRP = 512
CSET = 128
NB = 4096
CAP = 9
N_ROW = 32
N_COL = 8


def draw_block_rows(key, part):
    total_devices = N_ROW * N_COL
    entries = N_ROW * CAP
    dest_of_entry = jnp.arange(entries, dtype=jnp.int32) // CAP
    hot_dest = jax.random.randint(jax.random.fold_in(key, 13), (N_COL,), 0, N_ROW).astype(jnp.int32)
    device_keys = jax.random.split(jax.random.fold_in(key, 17), total_devices)
    ranks = jax.vmap(lambda one_key: jax.random.permutation(one_key, entries))(device_keys).astype(jnp.int32)
    col_of_device = jnp.arange(total_devices, dtype=jnp.int32) % N_COL
    is_hot = (dest_of_entry[None, :] == hot_dest[col_of_device][:, None]).astype(jnp.int32)
    scores = ranks - entries * is_hot
    order = jnp.argsort(scores, axis=1, stable=True)[:, :BLK_DEV]
    dests = dest_of_entry[order]
    inner = jax.random.randint(jax.random.fold_in(key, 11), (total_devices, BLK_DEV), 0, OWN_DEV).astype(jnp.int32)
    local_rows = dests * OWN_DEV + inner
    result = col_of_device[:, None] * RGRP + local_rows
    return result.reshape(N_ROW, N_COL, BLK_DEV).astype(jnp.int32)


def draw_block_cols(key, part):
    local_cols = jax.random.randint(jax.random.fold_in(key, 23), (N_ROW, N_COL, BLK_DEV), 0, CSET)
    owner = jnp.arange(N_ROW, dtype=jnp.int32)[:, None, None]
    return (local_cols // OWN_DEV * RGRP + owner * OWN_DEV + local_cols % OWN_DEV).astype(jnp.int32)


def draw_block_counts(key, part):
    total_devices = N_ROW * N_COL
    base = jax.random.randint(jax.random.fold_in(key, 31), (total_devices,), BLK_DEV // 4, BLK_DEV + 1)
    fullest = jax.random.randint(jax.random.fold_in(key, 37), (), 0, total_devices)
    base = jnp.where(jnp.arange(total_devices) == fullest, BLK_DEV, base)
    return base.reshape(N_ROW, N_COL).astype(jnp.int32)


def draw_precond(key, part):
    eye = jnp.eye(BS, dtype=jnp.float32)
    noise = jax.random.normal(jax.random.fold_in(key, 47), (N_COL, RGRP, BS, BS), jnp.float32)
    return (0.8 * eye + 0.15 * noise / jnp.sqrt(BS * 1.0)).astype(jnp.float32)


def shard_levels(own_key, shape, cuts, smallest, largest):
    gain = 1.0
    for position, parts in cuts:
        draws = jax.random.uniform(jax.random.fold_in(jax.random.fold_in(own_key, 6), position), (parts,), jnp.float32, smallest / len(cuts), largest / len(cuts))
        gain = gain * jnp.repeat(jnp.exp(draws), shape[position] // parts).reshape((-1,) + (1,) * (len(shape) - 1 - position))
    return gain


def scatter_about(stream_key, shape, width, bound, pieces=(), kind=jnp.bfloat16):
    array = width * jax.random.normal(stream_key, shape, jnp.float32)
    if pieces:
        array = array * shard_levels(stream_key, shape, pieces, -0.22, 0.18)
    return jnp.clip(array, -bound, bound).astype(kind)


def setup_inputs(seed: int = 0) -> dict:
    arg_keys = jax.random.split(jax.random.key(seed), 7)
    block_values = scatter_about(arg_keys[0], (N_ROW, N_COL, BLK_DEV, BS, BS), (7 * BS * BLK_DEV // OWN_DEV) ** -0.5, 0.0625, ((0, 32), (1, 8)))
    block_rows = draw_block_rows(jax.random.fold_in(arg_keys[6], 71), 0)
    block_cols = draw_block_cols(jax.random.fold_in(arg_keys[6], 71), 0)
    block_counts = draw_block_counts(jax.random.fold_in(arg_keys[6], 71), 0)
    precond = draw_precond(jax.random.fold_in(arg_keys[6], 71), 0)
    right_side = scatter_about(arg_keys[5], (N_COL, RGRP, RHS, BS), 1.0, 6.0, ((0, 8), (1, 32)), jnp.float32)
    return {"block_values": block_values, "block_rows": block_rows, "block_cols": block_cols, "block_counts": block_counts, "precond": precond, "right_side": right_side}


def apply_blocks(matrix, field):
    return jnp.einsum("poi,pki->pko", matrix.astype(jnp.float32), field.astype(jnp.float32), precision=lax.Precision.HIGHEST)


def reference(block_values, block_rows, block_cols, block_counts, precond, right_side):
    total_devices = N_ROW * N_COL
    rhs_flat = right_side.reshape(NB, RHS, BS).astype(jnp.float32)
    inverse = precond.reshape(NB, BS, BS).astype(jnp.float32)
    values = block_values.reshape(total_devices, BLK_DEV, BS, BS)
    rows = block_rows.reshape(total_devices, BLK_DEV).astype(jnp.int32)
    cols = block_cols.reshape(total_devices, BLK_DEV).astype(jnp.int32)
    counts = block_counts.reshape(total_devices).astype(jnp.int32)
    slot_ids = jnp.arange(BLK_DEV, dtype=jnp.int32)
    solution = apply_blocks(inverse, rhs_flat)
    for step in range(ITERS):
        rounded = lax.optimization_barrier(solution.astype(jnp.bfloat16)).astype(jnp.float32)

        def add_device(accum, inputs):
            vals, rr, cc, count = inputs
            xg = rounded[cc]
            contrib = jnp.einsum("soi,ski->sko", vals.astype(jnp.float32), xg)
            contrib = jnp.where((slot_ids < count)[:, None, None], contrib, jnp.zeros_like(contrib))
            return accum.at[rr].add(contrib), None

        product, _ = lax.scan(add_device, jnp.zeros((NB, RHS, BS), jnp.float32), (values, rows, cols, counts))
        residual = rhs_flat - solution - product
        solution = solution + apply_blocks(inverse, residual)
    return solution.reshape(N_COL, RGRP, RHS, BS)
```

```python
import functools

import jax
import jax.numpy as jnp
from jax import lax
from jax.experimental import pallas as pl
from jax.experimental.pallas import tpu as pltpu
from jax.sharding import PartitionSpec as P

ITERS = 3
GROUPS = 2
CHUNK = 48
WIDE = 2
MESH = pl.DeviceIdType.MESH
F32 = jnp.float32
BF16 = jnp.bfloat16


def tables(rows, cols, count, group, owned):
    slots = rows.shape[0]
    me = lax.axis_index("row")
    my_x, my_y, my_core = me // 8, (me // 2) % 4, me % 2
    local = rows % group
    dest, inner = local // owned, local % owned
    to_x, to_y, to_core = dest // 8, (dest // 2) % 4, dest % 2
    part, block = inner // 8, inner % 8
    gray = lambda v: v ^ (v >> 1)
    off_x, off_y = gray(to_x) ^ gray(my_x), gray(to_y) ^ gray(my_y)
    bits = off_x % 2 + 2 * (off_y % 2) + 4 * (off_x // 2) + 8 * (off_y // 2)
    place = jnp.zeros_like(dest)
    for stage in range(4):
        dim = (to_core + stage + 2 * part) % 4
        place = 2 * place + ((bits >> dim) & 1)
    own = (to_core == my_core).astype(jnp.int32)
    key = ((own * 2 + part) * 16 + place) * 8 + block
    ids = jnp.arange(slots, dtype=jnp.int32)
    key = jnp.where(ids < count, key, 512)
    full = key * 256 + ids
    rank = jnp.sum((full[None, :] < full[:, None]).astype(jnp.int32), axis=1)
    hot = rank[None, :] == ids[:, None]
    col_local = cols // group * owned + cols % owned
    pick = lambda v: jnp.sum(jnp.where(hot, v[None, :], 0), axis=1)
    slot_sorted, col_sorted, key_sorted = pick(ids), pick(col_local), pick(key)
    before = jnp.concatenate([jnp.full((1,), -1, jnp.int32), key_sorted[:-1]])
    keep = (key_sorted == before).astype(F32)
    places = jnp.arange(512, dtype=jnp.int32)
    upto = jnp.sum((key[None, :] <= places[:, None]).astype(jnp.int32), axis=1)
    here = jnp.sum((key[None, :] == places[:, None]).astype(jnp.int32), axis=1)
    last = jnp.where(here > 0, upto - 1, slots)
    return slot_sorted, col_sorted, keep, last


def kernel(slot, col, keep, last, values, precond, rhs, out,
           blocks, weights, xall, xuse, sums, osend, orecv, hsend, hrecv, wsend, wrecv,
           load_sem, ag_send, ag_recv, o_send, o_recv, h_send, h_recv):
    slots = values.shape[0]
    owned, wide = rhs.shape[0], rhs.shape[1]
    k = wide // GROUPS
    row, z = lax.axis_index("row"), lax.axis_index("col")
    x, y, core = row // 8, (row // 2) % 4, row % 2
    zr, zl = (z + 1) % 8, (z + 7) % 8

    def torus(dim):
        is_x, is_a = 1 - dim % 2, 1 - dim // 2
        nx = x + is_x * (is_a * (1 - 2 * (x % 2)) + (1 - is_a) * (3 - 2 * x))
        ny = y + (1 - is_x) * (is_a * (1 - 2 * (y % 2)) + (1 - is_a) * (3 - 2 * y))
        return ((nx * 4 + ny) * 2 + core, z)

    right, left = (row, zr), (row, zl)
    twin = ((x * 4 + y) * 2 + 1 - core, z)

    load = pltpu.make_async_copy(values, blocks, load_sem)
    load.start()

    barrier = pltpu.get_barrier_semaphore()
    for peer in (right, left, twin, torus(0), torus(1), torus(2), torus(3)):
        pl.semaphore_signal(barrier, inc=1, device_id=peer, device_id_type=MESH)

    def ring(n, g, way, hop):
        if way == 0:
            owner, peer = (z + 8 - (hop - 1)) % 8, right
        else:
            owner, peer = (z + (hop - 1)) % 8, left
        ref = xall.at[n, g, owner]
        if hop == 4:
            ref = ref.at[pl.ds(8 * way, 8)]
        return pltpu.make_async_remote_copy(
            src_ref=ref, dst_ref=ref,
            send_sem=ag_send.at[n, g, way, hop - 1], recv_sem=ag_recv.at[n, g, way, hop - 1],
            device_id=peer, device_id_type=MESH)

    def ring_in(n, g, way, hop):
        owner = (z + 8 - hop) % 8 if way == 0 else (z + hop) % 8
        ref = xall.at[n, g, owner]
        if hop == 4:
            ref = ref.at[pl.ds(8 * way, 8)]
        peer = right if way == 0 else left
        return pltpu.make_async_remote_copy(
            src_ref=ref, dst_ref=ref,
            send_sem=ag_send.at[n, g, way, hop - 1], recv_sem=ag_recv.at[n, g, way, hop - 1],
            device_id=peer, device_id_type=MESH)

    def twin_copy(n, g):
        return pltpu.make_async_remote_copy(
            src_ref=osend.at[g], dst_ref=orecv.at[n % 2, g],
            send_sem=o_send.at[n, g], recv_sem=o_recv.at[n, g],
            device_id=twin, device_id_type=MESH)

    def half_copy(n, g, m, t):
        h = 8 >> t
        source, target = (wsend, wrecv) if t >= WIDE else (hsend, hrecv)
        return pltpu.make_async_remote_copy(
            src_ref=source.at[g, m, pl.ds(h, h)], dst_ref=target.at[n, g, m, pl.ds(h, h)],
            send_sem=h_send.at[n, g, m, t], recv_sem=h_recv.at[n, g, m, t],
            device_id=torus((core + t + 2 * m) % 4), device_id_type=MESH)

    def apply(r, b):
        hi = r.astype(BF16)
        lo = (r - hi.astype(F32)).astype(BF16)
        both = lax.dot_general(jnp.concatenate([hi, lo], 0), weights[b],
                               (((1,), (0,)), ((), ())), preferred_element_type=F32)
        return both[:k, :128] + (both[:k, 128:] + both[k:, :128])

    def start_ring(n, g):
        ring(n, g, 0, 1).start()
        ring(n, g, 1, 1).start()

    for b in range(owned):
        turned = precond[b].T
        hi = turned.astype(BF16)
        lo = (turned - hi.astype(F32)).astype(BF16)
        weights[b] = jnp.concatenate([hi, lo], 1)
    for g in range(GROUPS):
        span = pl.ds(g * k, k)
        for b in range(owned):
            first = apply(rhs[b, span, :], b)
            out[b, span, :] = first
            xall[0, g, z, b] = first.astype(BF16)
        sums[g, slots] = jnp.zeros((k, 128), F32)
    pl.semaphore_wait(barrier, 7)
    for g in range(GROUPS):
        start_ring(0, g)
    load.wait()

    def products(g, first, count):
        def dots(c, carry):
            for u in range(0, CHUNK, 2):
                s = c * CHUNK + u
                pair = jnp.concatenate([blocks[slot[s]], blocks[slot[s + 1]]], 0)
                field = jnp.concatenate([xuse[g, col[s]], xuse[g, col[s + 1]]], 0)
                r = lax.dot_general(field, pair, (((1,), (1,)), ((), ())), preferred_element_type=F32)
                sums[g, s] = r[:k, :128]
                sums[g, s + 1] = r[k:, 128:]
            return carry

        lax.fori_loop(first, first + count, dots, 0)

    def running(g, first, count, carry):
        def step(c, total):
            for u in range(16):
                s = c * 16 + u
                total = sums[g, s] + keep[s] * total
                sums[g, s] = total
            return total

        return lax.fori_loop(first, first + count, step, carry)

    def total_of(n, g, m, d, b, stages):
        v = sums[g, last[256 + (m * 16 + d) * 8 + b]] + orecv[n % 2, g, m * 16 + d, b]
        for t in range(stages):
            source = wrecv if t >= WIDE else hrecv
            v = v + source[n, g, m, (8 >> t) + d, b].astype(F32)
        return v

    def iteration(n, carry):
        for hop in range(1, 4):
            for g in range(GROUPS):
                for way in range(2):
                    ring_in(n, g, way, hop).wait_recv()
                    ring(n, g, way, hop + 1).start()
        for g in range(GROUPS):
            for way in range(2):
                ring_in(n, g, way, 4).wait_recv()

            def take(c, a):
                for b in range(owned):
                    xuse[g, c * owned + b] = xall[n, g, c, b]
                return a

            lax.fori_loop(0, 8, take, 0)
            products(g, 0, 3)
            run = running(g, 0, 9, jnp.zeros((k, 128), F32))

            def other(c, a):
                for b in range(8):
                    osend[g, c, b] = sums[g, last[c * 8 + b]]
                return a

            lax.fori_loop(0, 32, other, 0)
            twin_copy(n, g).start()
            products(g, 3, 1)
            running(g, 9, 3, run)
        for t in range(4):
            for g in range(GROUPS):
                if t == 0:
                    twin_copy(n, g).wait_recv()
                for m in range(2):
                    if t > 0:
                        half_copy(n, g, m, t - 1).wait_recv()

                    def send(d, a):
                        for b in range(8):
                            v = total_of(n, g, m, d, b, t)
                            if t >= WIDE:
                                wsend[g, m, d, b] = v
                            else:
                                hsend[g, m, d, b] = v.astype(BF16)
                        return a

                    lax.fori_loop(8 >> t, 16 >> t, send, 0)
                    half_copy(n, g, m, t).start()
        for g in range(GROUPS):
            span = pl.ds(g * k, k)
            for m in range(2):
                half_copy(n, g, m, 3).wait_recv()
            for b in range(owned):
                now = out[b, span, :]
                residual = rhs[b, span, :] - now - total_of(n, g, b // 8, 0, b % 8, 4)
                now = now + apply(residual, b)
                out[b, span, :] = now

                @pl.when(n < ITERS - 1)
                def _():
                    xall[n + 1, g, z, b] = now.astype(BF16)

            @pl.when(n < ITERS - 1)
            def _():
                start_ring(n + 1, g)

        for g in range(GROUPS):
            for way in range(2):
                for hop in range(1, 5):
                    ring(n, g, way, hop).wait_send()
            twin_copy(n, g).wait_send()
            for m in range(2):
                for t in range(4):
                    half_copy(n, g, m, t).wait_send()
        return carry

    lax.fori_loop(0, ITERS, iteration, 0)


def per_device(block_values, block_rows, block_cols, block_counts, precond, right_side):
    owned, wide, bs = right_side.shape[1:]
    slots = block_values.shape[2]
    group = owned * lax.axis_size("row")
    k = wide // GROUPS
    index = tables(block_rows[0, 0], block_cols[0, 0], block_counts[0, 0], group, owned)
    vmem = pl.BlockSpec(memory_space=pltpu.VMEM)
    smem = pl.BlockSpec(memory_space=pltpu.SMEM)
    dma = pltpu.SemaphoreType.DMA
    result = pl.pallas_call(
        kernel,
        out_shape=jax.ShapeDtypeStruct((owned, wide, bs), F32),
        in_specs=[smem] * 4 + [pl.BlockSpec(memory_space=pl.ANY), vmem, vmem],
        out_specs=vmem,
        scratch_shapes=[
            pltpu.VMEM((slots, bs, bs), BF16),
            pltpu.VMEM((owned, bs, 2 * bs), BF16),
            pltpu.VMEM((ITERS, GROUPS, 8, owned, k, bs), BF16),
            pltpu.VMEM((GROUPS, 8 * owned, k, bs), BF16),
            pltpu.VMEM((GROUPS, slots + 1, k, bs), F32),
            pltpu.VMEM((GROUPS, 32, 8, k, bs), F32),
            pltpu.VMEM((2, GROUPS, 32, 8, k, bs), F32),
            pltpu.VMEM((GROUPS, 2, 16, 8, k, bs), BF16),
            pltpu.VMEM((ITERS, GROUPS, 2, 16, 8, k, bs), BF16),
            pltpu.VMEM((GROUPS, 2, 16 >> WIDE, 8, k, bs), F32),
            pltpu.VMEM((ITERS, GROUPS, 2, 16 >> WIDE, 8, k, bs), F32),
            dma,
            dma((ITERS, GROUPS, 2, 4)), dma((ITERS, GROUPS, 2, 4)),
            dma((ITERS, GROUPS)), dma((ITERS, GROUPS)),
            dma((ITERS, GROUPS, 2, 4)), dma((ITERS, GROUPS, 2, 4)),
        ],
        compiler_params=pltpu.CompilerParams(
            collective_id=0, has_side_effects=True, vmem_limit_bytes=58 << 20),
    )(*index, block_values[0, 0], precond[0], right_side[0])
    return result[None]


def solution(mesh):
    placed = (
        P("row", "col", None, None, None),
        P("row", "col", None),
        P("row", "col", None),
        P("row", "col"),
        P("col", "row", None, None),
        P("col", "row", None, None),
    )
    return jax.shard_map(
        per_device,
        mesh=mesh,
        in_specs=placed,
        out_specs=P("col", "row", None, None),
        check_vma=False,
    )
```

```python
import functools

import jax
import jax.numpy as jnp
from jax import lax
from jax.experimental import pallas as pl
from jax.experimental.pallas import tpu as pltpu
from jax.sharding import PartitionSpec as P

ITERS = 3
GROUPS = 2
CHUNK = 48
RINGP = 2
RINGB = 8
WIDE = 2
MESH = pl.DeviceIdType.MESH
F32 = jnp.float32
BF16 = jnp.bfloat16


def tables(rows, cols, count, group, owned):
    slots = rows.shape[0]
    me = lax.axis_index("row")
    my_x, my_y, my_core = me // 8, (me // 2) % 4, me % 2
    local = rows % group
    dest, inner = local // owned, local % owned
    to_x, to_y, to_core = dest // 8, (dest // 2) % 4, dest % 2
    part, block = inner // 8, inner % 8
    gray = lambda v: v ^ (v >> 1)
    off_x, off_y = gray(to_x) ^ gray(my_x), gray(to_y) ^ gray(my_y)
    bits = off_x % 2 + 2 * (off_y % 2) + 4 * (off_x // 2) + 8 * (off_y // 2)
    place = jnp.zeros_like(dest)
    for stage in range(4):
        dim = (to_core + stage + 2 * part) % 4
        place = 2 * place + ((bits >> dim) & 1)
    own = (to_core == my_core).astype(jnp.int32)
    key = ((own * 2 + part) * 16 + place) * 8 + block
    ids = jnp.arange(slots, dtype=jnp.int32)
    key = jnp.where(ids < count, key, 512)
    full = key * 256 + ids
    rank = jnp.sum((full[None, :] < full[:, None]).astype(jnp.int32), axis=1)
    hot = rank[None, :] == ids[:, None]
    col_local = cols // group * owned + cols % owned
    pick = lambda v: jnp.sum(jnp.where(hot, v[None, :], 0), axis=1)
    slot_sorted, col_sorted, key_sorted = pick(ids), pick(col_local), pick(key)
    before = jnp.concatenate([jnp.full((1,), -1, jnp.int32), key_sorted[:-1]])
    keep = (key_sorted == before).astype(F32)
    places = jnp.arange(512, dtype=jnp.int32)
    upto = jnp.sum((key[None, :] <= places[:, None]).astype(jnp.int32), axis=1)
    here = jnp.sum((key[None, :] == places[:, None]).astype(jnp.int32), axis=1)
    last = jnp.where(here > 0, upto - 1, slots)
    return slot_sorted, col_sorted, keep, last


def kernel(slot, col, keep, last, values, precond, rhs, out,
           blocks, turned, weights, sums, raw, wsend, wrecv, *rest):
    slots = values.shape[0]
    owned, k = rhs.shape[0], rhs.shape[1] // GROUPS
    rest = list(rest)
    take = lambda count: [rest.pop(0) for _ in range(count)]
    table = lambda: [take(GROUPS) for _ in range(ITERS)]
    xall, osend, orecv, hrecv = table(), table(), table(), table()
    hsend = take(GROUPS)
    load_sem, ag_send, ag_recv, o_send, o_recv, h_send, h_recv = rest
    row, z = lax.axis_index("row"), lax.axis_index("col")
    x, y, core = row // 8, (row // 2) % 4, row % 2

    def torus(dim):
        is_x, is_a = 1 - dim % 2, 1 - dim // 2
        nx = x + is_x * (is_a * (1 - 2 * (x % 2)) + (1 - is_a) * (3 - 2 * x))
        ny = y + (1 - is_x) * (is_a * (1 - 2 * (y % 2)) + (1 - is_a) * (3 - 2 * y))
        return nx, ny

    def beside(dim):
        px, py = torus(dim)
        return ((px * 4 + py) * 2 + core, z)

    def along(way, step):
        return (row, (z + step) % 8 if way == 0 else (z + 8 - step) % 8)

    def across(dim, other):
        (px, py), (qx, qy) = torus(dim), torus(other)
        flip = dim % 2
        return ((((1 - flip) * px + flip * qx) * 4 + (flip * py + (1 - flip) * qy)) * 2 + core, z)

    twin = ((x * 4 + y) * 2 + 1 - core, z)

    load = pltpu.make_async_copy(values, blocks, load_sem)
    load.start()

    barrier = pltpu.get_barrier_semaphore()
    for peer in (along(0, 1), along(1, 1), along(0, 2), along(1, 2), twin, beside(0), beside(1), beside(2), beside(3),
                 across((core + 2) % 4, (core + 3) % 4), across(core, (core + 1) % 4)):
        pl.semaphore_signal(barrier, inc=1, device_id=peer, device_id_type=MESH)

    def ring(n, g, way, far, part, incoming=False):
        back = far if incoming else (0 if far < 3 else 2)
        owner = (z + 8 - back) % 8 if way == 0 else (z + back) % 8
        ref = xall[n][g].at[owner, pl.ds(RINGB * part, RINGB)]
        return pltpu.make_async_remote_copy(
            src_ref=ref, dst_ref=ref,
            send_sem=ag_send.at[n, g, way, far - 1, part], recv_sem=ag_recv.at[n, g, way, far - 1, part],
            device_id=along(way, 2 - far % 2), device_id_type=MESH)

    def twin_copy(n, g, m, part):
        span = pl.ds(m * 16 + 8 * (1 - part), 8)
        return pltpu.make_async_remote_copy(
            src_ref=osend[n][g].at[span], dst_ref=orecv[n][g].at[span],
            send_sem=o_send.at[n, g, m, part], recv_sem=o_recv.at[n, g, m, part],
            device_id=twin, device_id_type=MESH)

    def is_wide(n, t):
        return n == ITERS - 1 and t >= WIDE

    def half_copy(n, g, m, t, d):
        source, target = (wsend.at[g], wrecv.at[g]) if is_wide(n, t) else (hsend[g], hrecv[n][g])
        dim = (core + t + 2 * m) % 4
        after = (dim + 1) % 4
        if t < 2:
            peer = beside(dim)
        else:
            peer = (None, beside(after), beside(dim), across(dim, after))[d]
        return pltpu.make_async_remote_copy(
            src_ref=source.at[m, d], dst_ref=target.at[m, d],
            send_sem=h_send.at[n, g, m, d], recv_sem=h_recv.at[n, g, m, d],
            device_id=peer, device_id_type=MESH)

    def apply(r, b):
        hi = r.astype(BF16)
        lo = (r - hi.astype(F32)).astype(BF16)
        both = lax.dot_general(jnp.concatenate([hi, lo], 0), weights[b],
                               (((1,), (0,)), ((), ())), preferred_element_type=F32)
        return both[:k, :128] + (both[:k, 128:] + both[k:, :128])

    def start_ring(n, g, part):
        for way in range(2):
            ring(n, g, way, 2, part).start()
        if part == RINGP - 1:
            for each in range(RINGP):
                for way in range(2):
                    ring(n, g, way, 1, each).start()

    def put(n, g, b, value):
        out[b, pl.ds(g * k, k), :] = value
        if n < ITERS:
            xall[n][g][z, b] = value.astype(BF16)
            if b % RINGB == RINGB - 1:
                start_ring(n, g, b // RINGB)

    for b in range(owned):
        flat = precond[b].T
        hi = flat.astype(BF16)
        lo = (flat - hi.astype(F32)).astype(BF16)
        weights[b] = jnp.concatenate([hi, lo], 1)
    pl.semaphore_wait(barrier, 11)
    for g in range(GROUPS):
        for b in range(owned):
            put(0, g, b, apply(rhs[b, pl.ds(g * k, k), :], b))
        sums[g, slots] = jnp.zeros((k, 128), F32)
    load.wait()

    def turn(first, count):
        def step(c, a):
            for u in range(8):
                turned[c * 8 + u] = blocks[c * 8 + u].T
            return a

        lax.fori_loop(first, first + count, step, 0)

    def products(n, g, first, count, carry):
        def dots(c, total):
            for u in range(0, CHUNK, 2):
                s = c * CHUNK + u
                pair = jnp.concatenate([turned[slot[s]], turned[slot[s + 1]]], 1)
                ca, cb = col[s], col[s + 1]
                field = jnp.concatenate([xall[n][g][ca // 16, ca % 16], xall[n][g][cb // 16, cb % 16]], 0)
                r = lax.dot_general(field, pair, (((1,), (0,)), ((), ())), preferred_element_type=F32)
                raw[u] = r[:k, :128]
                raw[u + 1] = r[k:, 128:]
            for u in range(CHUNK):
                s = c * CHUNK + u
                total = raw[u] + keep[s] * total
                sums[g, s] = total
            return total

        return lax.fori_loop(first, first + count, dots, carry)

    def total_of(n, g, m, d, b, stages, final=False):
        v = sums[g, last[256 + (m * 16 + d) * 8 + b]] + orecv[n][g][m * 16 + d, b].astype(F32)
        for t in range(stages):
            v = v + hrecv[n][g][m, (8 >> t) + d, b].astype(F32)
        for e in range(1, 4 if final else 1):
            v = v + (wrecv[g, m, e, b] if is_wide(n, 2) else hrecv[n][g][m, e, b].astype(F32))
        return v

    def on_last(way, part):
        return part // (RINGP // 2) == way

    def relay(n, g):
        for part in range(RINGP):
            for way in range(2):
                ring(n, g, way, 2, part, True).wait_recv()
                ring(n, g, way, 3, part).start()
                if on_last(way, part):
                    ring(n, g, way, 4, part).start()

    def gathered(n, g):
        for far in (1, 3, 4):
            for part in range(RINGP):
                for way in range(2):
                    if far < 4 or on_last(way, part):
                        ring(n, g, way, far, part, True).wait_recv()

    def compute(n, g):
        run = products(n, g, 0, 3, jnp.zeros((k, 128), F32))
        for part in range(2):
            for m in range(2):
                def other(c, a):
                    for b in range(8):
                        osend[n][g][c, b] = sums[g, last[c * 8 + b]].astype(osend[n][g].dtype)
                    return a

                first = m * 16 + 8 * (1 - part)
                lax.fori_loop(first, first + 8, other, 0)
                twin_copy(n, g, m, part).start()
        products(n, g, 3, 1, run)

    def exchange(n, g, t):
        top = 16 >> t

        def send(i, a):
            d = top - 1 - i
            for m in range(2):
                if n > 0 and not is_wide(n, t):
                    half_copy(n - 1, g, m, t, d).wait_send()
                for s in range(t):
                    half_copy(n, g, m, s, (8 >> s) + d).wait_recv()
                for b in range(8):
                    v = total_of(n, g, m, d, b, t)
                    if is_wide(n, t):
                        wsend[g, m, d, b] = v
                    else:
                        hsend[g][m, d, b] = v.astype(BF16)
                half_copy(n, g, m, t, d).start()
            return a

        if t < 2:
            for m in range(2):
                twin_copy(n, g, m, t).wait_recv()
            lax.fori_loop(0, 8 >> t, send, 0)
        else:
            for i in range(3):
                send(i, 0)

    def update(n, g):
        for m in range(2):
            for t, d in ((0, 8), (1, 4), (2, 3), (2, 2), (2, 1)):
                half_copy(n, g, m, t, d).wait_recv()
            for b in range(8 * m, 8 * m + 8):
                now = out[b, pl.ds(g * k, k), :]
                residual = rhs[b, pl.ds(g * k, k), :] - now - total_of(n, g, m, 0, b % 8, 2, True)
                put(n + 1, g, b, now + apply(residual, b))

    turn(0, 12)
    for n in range(ITERS):
        if n > 0:
            exchange(n - 1, 1, 0)
        relay(n, 0)
        if n > 0:
            exchange(n - 1, 1, 1)
            exchange(n - 1, 1, 2)
        else:
            turn(12, 12)
        gathered(n, 0)
        compute(n, 0)
        if n > 0:
            update(n - 1, 1)
        exchange(n, 0, 0)
        relay(n, 1)
        exchange(n, 0, 1)
        exchange(n, 0, 2)
        gathered(n, 1)
        compute(n, 1)
        update(n, 0)
    for t in range(3):
        exchange(ITERS - 1, 1, t)
    update(ITERS - 1, 1)

    for n in range(ITERS):
        for g in range(GROUPS):
            for way in range(2):
                for far in range(1, 5):
                    for part in range(RINGP):
                        if far < 4 or on_last(way, part):
                            ring(n, g, way, far, part).wait_send()
            for m in range(2):
                for part in range(2):
                    twin_copy(n, g, m, part).wait_send()
                for t, places in enumerate((range(8, 16), range(4, 8), range(1, 4))):
                    for d in places:
                        if n == ITERS - 1 or is_wide(n + 1, t):
                            half_copy(n, g, m, t, d).wait_send()


def per_device(block_values, block_rows, block_cols, block_counts, precond, right_side):
    owned, wide, bs = right_side.shape[1:]
    slots = block_values.shape[2]
    group = owned * lax.axis_size("row")
    k = wide // GROUPS
    index = tables(block_rows[0, 0], block_cols[0, 0], block_counts[0, 0], group, owned)
    vmem = pl.BlockSpec(memory_space=pltpu.VMEM)
    smem = pl.BlockSpec(memory_space=pltpu.SMEM)
    dma = pltpu.SemaphoreType.DMA
    result = pl.pallas_call(
        kernel,
        out_shape=jax.ShapeDtypeStruct((owned, wide, bs), F32),
        in_specs=[smem] * 4 + [pl.BlockSpec(memory_space=pl.ANY), vmem, vmem],
        out_specs=vmem,
        scratch_shapes=[
            pltpu.VMEM((slots, bs, bs), BF16),
            pltpu.VMEM((slots, bs, bs), BF16),
            pltpu.VMEM((owned, bs, 2 * bs), BF16),
            pltpu.VMEM((GROUPS, slots + 1, k, bs), F32),
            pltpu.VMEM((CHUNK, k, bs), F32)]
        + [pltpu.VMEM((GROUPS, 2, 16 >> WIDE, 8, k, bs), F32)] * 2
        + [pltpu.VMEM((8, owned, k, bs), BF16)] * (ITERS * GROUPS)
        + ([pltpu.VMEM((32, 8, k, bs), BF16)] * ((ITERS - 1) * GROUPS)
           + [pltpu.VMEM((32, 8, k, bs), F32)] * GROUPS) * 2
        + [pltpu.VMEM((2, 16, 8, k, bs), BF16)] * (GROUPS + ITERS * GROUPS)
        + [
            dma,
            dma((ITERS, GROUPS, 2, 4, RINGP)), dma((ITERS, GROUPS, 2, 4, RINGP)),
            dma((ITERS, GROUPS, 2, 2)), dma((ITERS, GROUPS, 2, 2)),
            dma((ITERS, GROUPS, 2, 16)), dma((ITERS, GROUPS, 2, 16)),
        ],
        compiler_params=pltpu.CompilerParams(
            collective_id=0, has_side_effects=True, vmem_limit_bytes=58 << 20),
    )(*index, block_values[0, 0], precond[0], right_side[0])
    return result[None]


def solution(mesh):
    placed = (
        P("row", "col", None, None, None),
        P("row", "col", None),
        P("row", "col", None),
        P("row", "col"),
        P("col", "row", None, None),
        P("col", "row", None, None),
    )
    return jax.shard_map(
        per_device,
        mesh=mesh,
        in_specs=placed,
        out_specs=P("col", "row", None, None),
        check_vma=False,
    )
```

```python
import jax
import jax.numpy as jnp
from jax import lax
from jax.experimental import pallas as pl
from jax.experimental.pallas import tpu as pltpu
from jax.sharding import PartitionSpec as P

ITERS = 3
GROUPS = 2
CHUNK = 48
RINGP = 2
RINGB = 8
WIDE = 2
MESH = pl.DeviceIdType.MESH
F32 = jnp.float32
BF16 = jnp.bfloat16


def tables(rows, cols, count, x, y, core, slots):
    total = lambda v, axis: jnp.sum(v.astype(jnp.int32), axis=axis, keepdims=True)
    wave = lambda shape, axis: lax.broadcasted_iota(jnp.int32, shape, axis)
    gray = lambda v: v ^ (v >> 1)
    local = rows & 511
    dest, inner = local >> 4, local & 15
    to_x, to_y, to_core = dest >> 3, (dest >> 1) & 3, dest & 1
    part, block = inner >> 3, inner & 7
    off_x = gray(to_x) ^ gray(jnp.full_like(rows, x))
    off_y = gray(to_y) ^ gray(jnp.full_like(rows, y))
    flags = (off_x & 1, off_y & 1, off_x >> 1, off_y >> 1)
    place = jnp.zeros_like(rows)
    for stage in range(4):
        dim = (to_core + stage + 2 * part) & 3
        bit = jnp.zeros_like(rows)
        for d in range(4):
            bit = jnp.where(dim == d, flags[d], bit)
        place = 2 * place + bit
    own = jnp.where(to_core == core, 1, 0)
    key = ((own * 2 + part) * 16 + place) * 8 + block
    ids = wave((1, slots), 1)
    key = jnp.where(ids < count, key, 512)
    full = key * 256 + ids
    near = (cols >> 9) * 16 + (cols & 15)
    eye = wave((slots, slots), 0) == wave((slots, slots), 1)
    upright = lambda v: total(jnp.where(eye, v, 0), 1)
    full_up, near_up = upright(full), upright(near)
    key_up, ids_up = full_up >> 8, full_up & 255
    rank = total(jnp.where(full < full_up, 1, 0), 1)
    lanes = wave((1, 512), 1)
    pick = lambda hot, v: total(jnp.where(hot, v, 0), 0)
    hot = rank == lanes
    slot, col, key_at = pick(hot, ids_up), pick(hot, near_up), pick(hot, key_up)
    keep = jnp.where(key_at == pick(rank + 1 == lanes, key_up), 1.0, 0.0)
    upto = total(jnp.where(key_up <= lanes, 1, 0), 0)
    here = total(jnp.where(key_up == lanes, 1, 0), 0)
    last = jnp.where(here > 0, upto - 1, slots)
    line = wave((8, 512), 0)
    return jnp.where(line == 0, slot, jnp.where(line == 1, col, last)), jnp.broadcast_to(keep, (8, 512))


def kernel(rows, cols, count, values, precond, rhs, out,
           blocks, turned, weights, sums, raw, wsend, wrecv, index_v, keep_v, index, keep, *rest):
    slots = values.shape[0]
    owned, k = rhs.shape[0], rhs.shape[1] // GROUPS
    rest = list(rest)
    take = lambda count: [rest.pop(0) for _ in range(count)]
    table = lambda: [take(GROUPS) for _ in range(ITERS)]
    xall, osend, orecv, hrecv = table(), table(), table(), table()
    hsend = take(GROUPS)
    load_sem, index_sem, keep_sem, ag_send, ag_recv, o_send, o_recv, h_send, h_recv = rest
    row, z = lax.axis_index("row"), lax.axis_index("col")
    x, y, core = row // 8, (row // 2) % 4, row % 2

    def torus(dim):
        is_x, is_a = 1 - dim % 2, 1 - dim // 2
        nx = x + is_x * (is_a * (1 - 2 * (x % 2)) + (1 - is_a) * (3 - 2 * x))
        ny = y + (1 - is_x) * (is_a * (1 - 2 * (y % 2)) + (1 - is_a) * (3 - 2 * y))
        return nx, ny

    def beside(dim):
        px, py = torus(dim)
        return ((px * 4 + py) * 2 + core, z)

    def along(way, step):
        return (row, (z + step) % 8 if way == 0 else (z + 8 - step) % 8)

    def across(dim, other):
        (px, py), (qx, qy) = torus(dim), torus(other)
        flip = dim % 2
        return ((((1 - flip) * px + flip * qx) * 4 + (flip * py + (1 - flip) * qy)) * 2 + core, z)

    twin = ((x * 4 + y) * 2 + 1 - core, z)

    load = pltpu.make_async_copy(values, blocks, load_sem)
    load.start()

    barrier = pltpu.get_barrier_semaphore()
    for peer in (along(0, 1), along(1, 1), along(0, 2), along(1, 2), twin, beside(0), beside(1), beside(2), beside(3),
                 across((core + 2) % 4, (core + 3) % 4), across(core, (core + 1) % 4)):
        pl.semaphore_signal(barrier, inc=1, device_id=peer, device_id_type=MESH)

    def ring(n, g, way, far, part, incoming=False):
        back = far if incoming else (0 if far < 3 else 2)
        owner = (z + 8 - back) % 8 if way == 0 else (z + back) % 8
        ref = xall[n][g].at[owner, pl.ds(RINGB * part, RINGB)]
        return pltpu.make_async_remote_copy(
            src_ref=ref, dst_ref=ref,
            send_sem=ag_send.at[n, g, way, far - 1, part], recv_sem=ag_recv.at[n, g, way, far - 1, part],
            device_id=along(way, 2 - far % 2), device_id_type=MESH)

    def twin_copy(n, g, m, part):
        span = pl.ds(m * 16 + 8 * (1 - part), 8)
        return pltpu.make_async_remote_copy(
            src_ref=osend[n][g].at[span], dst_ref=orecv[n][g].at[span],
            send_sem=o_send.at[n, g, m, part], recv_sem=o_recv.at[n, g, m, part],
            device_id=twin, device_id_type=MESH)

    def is_wide(n, t):
        return n == ITERS - 1 and t >= WIDE

    def half_copy(n, g, m, t, d):
        source, target = (wsend.at[g], wrecv.at[g]) if is_wide(n, t) else (hsend[g], hrecv[n][g])
        dim = (core + t + 2 * m) % 4
        after = (dim + 1) % 4
        if t < 2:
            peer = beside(dim)
        else:
            peer = (None, beside(after), beside(dim), across(dim, after))[d]
        return pltpu.make_async_remote_copy(
            src_ref=source.at[m, d], dst_ref=target.at[m, d],
            send_sem=h_send.at[n, g, m, d], recv_sem=h_recv.at[n, g, m, d],
            device_id=peer, device_id_type=MESH)

    def apply(r, b):
        hi = r.astype(BF16)
        lo = (r - hi.astype(F32)).astype(BF16)
        both = lax.dot_general(jnp.concatenate([hi, lo], 0), weights[b],
                               (((1,), (0,)), ((), ())), preferred_element_type=F32)
        return both[:k, :128] + (both[:k, 128:] + both[k:, :128])

    def start_ring(n, g, part):
        for way in range(2):
            ring(n, g, way, 2, part).start()
        if part == RINGP - 1:
            for each in range(RINGP):
                for way in range(2):
                    ring(n, g, way, 1, each).start()

    def put(n, g, b, value):
        out[b, pl.ds(g * k, k), :] = value
        if n < ITERS:
            xall[n][g][z, b] = value.astype(BF16)
            if b % RINGB == RINGB - 1:
                start_ring(n, g, b // RINGB)

    for b in range(owned):
        flat = precond[b].T
        hi = flat.astype(BF16)
        lo = (flat - hi.astype(F32)).astype(BF16)
        weights[b] = jnp.concatenate([hi, lo], 1)
    pl.semaphore_wait(barrier, 11)
    for g in range(GROUPS):
        for b in range(owned):
            put(0, g, b, apply(rhs[b, pl.ds(g * k, k), :], b))
        sums[g, slots] = jnp.zeros((k, 128), F32)
    index_v[...], keep_v[...] = tables(rows[...], cols[...], count[...], x, y, core, slots)
    moves = (pltpu.make_async_copy(index_v, index, index_sem), pltpu.make_async_copy(keep_v, keep, keep_sem))
    for move in moves:
        move.start()
    load.wait()

    def turn(first, count):
        def step(c, a):
            for u in range(8):
                turned[c * 8 + u] = blocks[c * 8 + u].T
            return a

        lax.fori_loop(first, first + count, step, 0)

    def products(n, g, first, count, carry):
        def dots(c, total):
            for u in range(0, CHUNK, 2):
                s = c * CHUNK + u
                pair = jnp.concatenate([turned[index[0, s]], turned[index[0, s + 1]]], 1)
                ca, cb = index[1, s], index[1, s + 1]
                field = jnp.concatenate([xall[n][g][ca // 16, ca % 16], xall[n][g][cb // 16, cb % 16]], 0)
                r = lax.dot_general(field, pair, (((1,), (0,)), ((), ())), preferred_element_type=F32)
                raw[u] = r[:k, :128]
                raw[u + 1] = r[k:, 128:]
            for u in range(CHUNK):
                s = c * CHUNK + u
                total = raw[u] + keep[0, s] * total
                sums[g, s] = total
            return total

        return lax.fori_loop(first, first + count, dots, carry)

    def total_of(n, g, m, d, b, stages, final=False):
        v = sums[g, index[2, 256 + (m * 16 + d) * 8 + b]] + orecv[n][g][m * 16 + d, b].astype(F32)
        for t in range(stages):
            v = v + hrecv[n][g][m, (8 >> t) + d, b].astype(F32)
        for e in range(1, 4 if final else 1):
            v = v + (wrecv[g, m, e, b] if is_wide(n, 2) else hrecv[n][g][m, e, b].astype(F32))
        return v

    def on_last(way, part):
        return part // (RINGP // 2) == way

    def relay(n, g):
        for part in range(RINGP):
            for way in range(2):
                ring(n, g, way, 2, part, True).wait_recv()
                ring(n, g, way, 3, part).start()
                if on_last(way, part):
                    ring(n, g, way, 4, part).start()

    def gathered(n, g):
        for far in (1, 3, 4):
            for part in range(RINGP):
                for way in range(2):
                    if far < 4 or on_last(way, part):
                        ring(n, g, way, far, part, True).wait_recv()

    def compute(n, g):
        run = products(n, g, 0, 3, jnp.zeros((k, 128), F32))
        for part in range(2):
            for m in range(2):
                def other(c, a):
                    for b in range(8):
                        osend[n][g][c, b] = sums[g, index[2, c * 8 + b]].astype(osend[n][g].dtype)
                    return a

                first = m * 16 + 8 * (1 - part)
                lax.fori_loop(first, first + 8, other, 0)
                twin_copy(n, g, m, part).start()
        products(n, g, 3, 1, run)

    def exchange(n, g, t):
        top = 16 >> t

        def send(i, a):
            d = top - 1 - i
            for m in range(2):
                if n > 0 and not is_wide(n, t):
                    half_copy(n - 1, g, m, t, d).wait_send()
                for s in range(t):
                    half_copy(n, g, m, s, (8 >> s) + d).wait_recv()
                for b in range(8):
                    v = total_of(n, g, m, d, b, t)
                    if is_wide(n, t):
                        wsend[g, m, d, b] = v
                    else:
                        hsend[g][m, d, b] = v.astype(BF16)
                half_copy(n, g, m, t, d).start()
            return a

        if t < 2:
            for m in range(2):
                twin_copy(n, g, m, t).wait_recv()
            lax.fori_loop(0, 8 >> t, send, 0)
        else:
            for i in range(3):
                send(i, 0)

    def update(n, g):
        for m in range(2):
            for t, d in ((0, 8), (1, 4), (2, 3), (2, 2), (2, 1)):
                half_copy(n, g, m, t, d).wait_recv()
            for b in range(8 * m, 8 * m + 8):
                now = out[b, pl.ds(g * k, k), :]
                residual = rhs[b, pl.ds(g * k, k), :] - now - total_of(n, g, m, 0, b % 8, 2, True)
                put(n + 1, g, b, now + apply(residual, b))

    turn(0, 12)
    for move in moves:
        move.wait()
    for n in range(ITERS):
        if n > 0:
            exchange(n - 1, 1, 0)
        relay(n, 0)
        if n > 0:
            exchange(n - 1, 1, 1)
            exchange(n - 1, 1, 2)
        else:
            turn(12, 12)
        gathered(n, 0)
        compute(n, 0)
        if n > 0:
            update(n - 1, 1)
        exchange(n, 0, 0)
        relay(n, 1)
        exchange(n, 0, 1)
        exchange(n, 0, 2)
        gathered(n, 1)
        compute(n, 1)
        update(n, 0)
    for t in range(3):
        exchange(ITERS - 1, 1, t)
    update(ITERS - 1, 1)

    for n in range(ITERS):
        for g in range(GROUPS):
            for way in range(2):
                for far in range(1, 5):
                    for part in range(RINGP):
                        if far < 4 or on_last(way, part):
                            ring(n, g, way, far, part).wait_send()
            for m in range(2):
                for part in range(2):
                    twin_copy(n, g, m, part).wait_send()
                for t, places in enumerate((range(8, 16), range(4, 8), range(1, 4))):
                    for d in places:
                        if n == ITERS - 1 or is_wide(n + 1, t):
                            half_copy(n, g, m, t, d).wait_send()


def per_device(block_values, block_rows, block_cols, block_counts, precond, right_side):
    owned, wide, bs = right_side.shape[1:]
    slots = block_values.shape[2]
    k = wide // GROUPS
    vmem = pl.BlockSpec(memory_space=pltpu.VMEM)
    dma = pltpu.SemaphoreType.DMA
    result = pl.pallas_call(
        kernel,
        out_shape=jax.ShapeDtypeStruct((owned, wide, bs), F32),
        in_specs=[vmem, vmem, vmem, pl.BlockSpec(memory_space=pl.ANY), vmem, vmem],
        out_specs=vmem,
        scratch_shapes=[
            pltpu.VMEM((slots, bs, bs), BF16),
            pltpu.VMEM((slots, bs, bs), BF16),
            pltpu.VMEM((owned, bs, 2 * bs), BF16),
            pltpu.VMEM((GROUPS, slots + 1, k, bs), F32),
            pltpu.VMEM((CHUNK, k, bs), F32)]
        + [pltpu.VMEM((GROUPS, 2, 16 >> WIDE, 8, k, bs), F32)] * 2
        + [pltpu.VMEM((8, 512), jnp.int32), pltpu.VMEM((8, 512), F32),
           pltpu.SMEM((8, 512), jnp.int32), pltpu.SMEM((8, 512), F32)]
        + [pltpu.VMEM((8, owned, k, bs), BF16)] * (ITERS * GROUPS)
        + ([pltpu.VMEM((32, 8, k, bs), BF16)] * ((ITERS - 1) * GROUPS)
           + [pltpu.VMEM((32, 8, k, bs), F32)] * GROUPS) * 2
        + [pltpu.VMEM((2, 16, 8, k, bs), BF16)] * (GROUPS + ITERS * GROUPS)
        + [
            dma, dma, dma,
            dma((ITERS, GROUPS, 2, 4, RINGP)), dma((ITERS, GROUPS, 2, 4, RINGP)),
            dma((ITERS, GROUPS, 2, 2)), dma((ITERS, GROUPS, 2, 2)),
            dma((ITERS, GROUPS, 2, 16)), dma((ITERS, GROUPS, 2, 16)),
        ],
        compiler_params=pltpu.CompilerParams(
            collective_id=0, has_side_effects=True, vmem_limit_bytes=58 << 20),
    )(block_rows[0], block_cols[0], block_counts, block_values[0, 0], precond[0], right_side[0])
    return result[None]


def solution(mesh):
    placed = (
        P("row", "col", None, None, None),
        P("row", "col", None),
        P("row", "col", None),
        P("row", "col"),
        P("col", "row", None, None),
        P("col", "row", None, None),
    )
    return jax.shard_map(
        per_device,
        mesh=mesh,
        in_specs=placed,
        out_specs=P("col", "row", None, None),
        check_vma=False,
    )
```

```python
import jax
import jax.numpy as jnp
from jax import lax
from jax.experimental import pallas as pl
from jax.experimental.pallas import tpu as pltpu
from jax.sharding import PartitionSpec as P

ITERS = 3
GROUPS = 2
CHUNK = 72
RINGP = 2
RINGB = 8
WIDE = 2
MESH = pl.DeviceIdType.MESH
F32 = jnp.float32
BF16 = jnp.bfloat16


def tables(rows, cols, count, x, y, core, slots):
    total = lambda v, axis: jnp.sum(v.astype(jnp.int32), axis=axis, keepdims=True)
    wave = lambda shape, axis: lax.broadcasted_iota(jnp.int32, shape, axis)
    gray = lambda v: v ^ (v >> 1)
    local = rows & 511
    dest, inner = local >> 4, local & 15
    to_x, to_y, to_core = dest >> 3, (dest >> 1) & 3, dest & 1
    part, block = inner >> 3, inner & 7
    off_x = gray(to_x) ^ gray(jnp.full_like(rows, x))
    off_y = gray(to_y) ^ gray(jnp.full_like(rows, y))
    flags = (off_x & 1, off_y & 1, off_x >> 1, off_y >> 1)
    place = jnp.zeros_like(rows)
    for stage in range(4):
        dim = (to_core + stage + 2 * part) & 3
        bit = jnp.zeros_like(rows)
        for d in range(4):
            bit = jnp.where(dim == d, flags[d], bit)
        place = 2 * place + bit
    own = jnp.where(to_core == core, 1, 0)
    key = ((own * 2 + part) * 16 + place) * 8 + block
    ids = wave((1, slots), 1)
    key = jnp.where(ids < count, key, 512)
    full = key * 256 + ids
    near = (cols >> 9) * 16 + (cols & 15)
    eye = wave((slots, slots), 0) == wave((slots, slots), 1)
    upright = lambda v: total(jnp.where(eye, v, 0), 1)
    full_up, near_up = upright(full), upright(near)
    key_up, ids_up = full_up >> 8, full_up & 255
    rank = total(jnp.where(full < full_up, 1, 0), 1)
    lanes = wave((1, 512), 1)
    pick = lambda hot, v: total(jnp.where(hot, v, 0), 0)
    hot = rank == lanes
    slot, col, key_at = pick(hot, ids_up), pick(hot, near_up), pick(hot, key_up)
    keep = jnp.where(key_at == pick(rank + 1 == lanes, key_up), 1.0, 0.0)
    upto = total(jnp.where(key_up <= lanes, 1, 0), 0)
    here = total(jnp.where(key_up == lanes, 1, 0), 0)
    last = jnp.where(here > 0, upto - 1, slots)
    line = wave((8, 512), 0)
    return jnp.where(line == 0, slot, jnp.where(line == 1, col, last)), jnp.broadcast_to(keep, (8, 512))


def kernel(rows, cols, count, values, precond, rhs, out,
           blocks, turned, weights, sums, raw, wsend, wrecv, index_v, keep_v, index, keep, *rest):
    slots = values.shape[0]
    owned, k = rhs.shape[0], rhs.shape[1] // GROUPS
    rest = list(rest)
    take = lambda count: [rest.pop(0) for _ in range(count)]
    table = lambda: [take(GROUPS) for _ in range(ITERS)]
    xall, osend, orecv, hrecv = table(), table(), table(), table()
    hsend = take(GROUPS)
    load_sem, index_sem, keep_sem, ag_send, ag_recv, o_send, o_recv, h_send, h_recv = rest
    row, z = lax.axis_index("row"), lax.axis_index("col")
    x, y, core = row // 8, (row // 2) % 4, row % 2

    def torus(dim):
        is_x, is_a = 1 - dim % 2, 1 - dim // 2
        nx = x + is_x * (is_a * (1 - 2 * (x % 2)) + (1 - is_a) * (3 - 2 * x))
        ny = y + (1 - is_x) * (is_a * (1 - 2 * (y % 2)) + (1 - is_a) * (3 - 2 * y))
        return nx, ny

    def beside(dim):
        px, py = torus(dim)
        return ((px * 4 + py) * 2 + core, z)

    def along(way, step):
        return (row, (z + step) % 8 if way == 0 else (z + 8 - step) % 8)

    def across(dim, other):
        (px, py), (qx, qy) = torus(dim), torus(other)
        flip = dim % 2
        return ((((1 - flip) * px + flip * qx) * 4 + (flip * py + (1 - flip) * qy)) * 2 + core, z)

    twin = ((x * 4 + y) * 2 + 1 - core, z)

    load = pltpu.make_async_copy(values, blocks, load_sem)
    load.start()

    barrier = pltpu.get_barrier_semaphore()
    for peer in (along(0, 1), along(1, 1), along(0, 2), along(1, 2), twin, beside(0), beside(1), beside(2), beside(3),
                 across((core + 2) % 4, (core + 3) % 4), across(core, (core + 1) % 4)):
        pl.semaphore_signal(barrier, inc=1, device_id=peer, device_id_type=MESH)

    def ring(n, g, way, far, part, incoming=False):
        back = far if incoming else (0 if far < 3 else 2)
        owner = (z + 8 - back) % 8 if way == 0 else (z + back) % 8
        ref = xall[n][g].at[owner, pl.ds(RINGB * part, RINGB)]
        return pltpu.make_async_remote_copy(
            src_ref=ref, dst_ref=ref,
            send_sem=ag_send.at[n, g, way, far - 1, part], recv_sem=ag_recv.at[n, g, way, far - 1, part],
            device_id=along(way, 2 - far % 2), device_id_type=MESH)

    def twin_copy(n, g, m, part):
        span = pl.ds(m * 16 + 8 * (1 - part), 8)
        return pltpu.make_async_remote_copy(
            src_ref=osend[n][g].at[span], dst_ref=orecv[n][g].at[span],
            send_sem=o_send.at[n, g, m, part], recv_sem=o_recv.at[n, g, m, part],
            device_id=twin, device_id_type=MESH)

    def is_wide(n, t):
        return n == ITERS - 1 and t >= WIDE

    def half_copy(n, g, m, t, d):
        source, target = (wsend.at[g], wrecv.at[g]) if is_wide(n, t) else (hsend[g], hrecv[n][g])
        dim = (core + t + 2 * m) % 4
        after = (dim + 1) % 4
        if t < 2:
            peer = beside(dim)
        else:
            peer = (None, beside(after), beside(dim), across(dim, after))[d]
        return pltpu.make_async_remote_copy(
            src_ref=source.at[m, d], dst_ref=target.at[m, d],
            send_sem=h_send.at[n, g, m, d], recv_sem=h_recv.at[n, g, m, d],
            device_id=peer, device_id_type=MESH)

    def apply(r, b):
        hi = r.astype(BF16)
        lo = (r - hi.astype(F32)).astype(BF16)
        both = lax.dot_general(jnp.concatenate([hi, lo], 0), weights[b],
                               (((1,), (0,)), ((), ())), preferred_element_type=F32)
        return both[:k, :128] + (both[:k, 128:] + both[k:, :128])

    def start_ring(n, g, part):
        for way in range(2):
            ring(n, g, way, 2, part).start()
        if part == RINGP - 1:
            for each in range(RINGP):
                for way in range(2):
                    ring(n, g, way, 1, each).start()

    def put(n, g, b, value):
        out[b, pl.ds(g * k, k), :] = value
        if n < ITERS:
            xall[n][g][z, b] = value.astype(BF16)
            if b % RINGB == RINGB - 1:
                start_ring(n, g, b // RINGB)

    for b in range(owned):
        flat = precond[b].T
        hi = flat.astype(BF16)
        lo = (flat - hi.astype(F32)).astype(BF16)
        weights[b] = jnp.concatenate([hi, lo], 1)
    pl.semaphore_wait(barrier, 11)

    def begin(g):
        for b in range(owned):
            put(0, g, b, apply(rhs[b, pl.ds(g * k, k), :], b))
        sums[g, slots] = jnp.zeros((k, 128), F32)

    begin(0)
    index_v[...], keep_v[...] = tables(rows[...], cols[...], count[...], x, y, core, slots)
    moves = (pltpu.make_async_copy(index_v, index, index_sem), pltpu.make_async_copy(keep_v, keep, keep_sem))
    for move in moves:
        move.start()
    load.wait()

    def turn(first, count):
        def step(c, a):
            for u in range(8):
                turned[c * 8 + u] = blocks[c * 8 + u].T
            return a

        lax.fori_loop(first, first + count, step, 0)

    def products(n, g, start, count, width, carry):
        def dots(c, total):
            for u in range(0, width, 2):
                s = start + c * width + u
                pair = jnp.concatenate([turned[index[0, s]], turned[index[0, s + 1]]], 1)
                ca, cb = index[1, s], index[1, s + 1]
                field = jnp.concatenate([xall[n][g][ca // 16, ca % 16], xall[n][g][cb // 16, cb % 16]], 0)
                r = lax.dot_general(field, pair, (((1,), (0,)), ((), ())), preferred_element_type=F32)
                raw[u] = r[:k, :128]
                raw[u + 1] = r[k:, 128:]
            for u in range(width):
                s = start + c * width + u
                total = raw[u] + keep[0, s] * total
                sums[g, s] = total
            return total

        return lax.fori_loop(0, count, dots, carry)

    def total_of(n, g, m, d, b, stages, final=False):
        v = sums[g, index[2, 256 + (m * 16 + d) * 8 + b]] + orecv[n][g][m * 16 + d, b].astype(F32)
        for t in range(stages):
            v = v + hrecv[n][g][m, (8 >> t) + d, b].astype(F32)
        for e in range(1, 4 if final else 1):
            v = v + (wrecv[g, m, e, b] if is_wide(n, 2) else hrecv[n][g][m, e, b].astype(F32))
        return v

    def on_last(way, part):
        return part // (RINGP // 2) == way

    def relay(n, g):
        for part in range(RINGP):
            for way in range(2):
                ring(n, g, way, 2, part, True).wait_recv()
                ring(n, g, way, 3, part).start()
                if on_last(way, part):
                    ring(n, g, way, 4, part).start()

    def gathered(n, g):
        for far in (1, 3, 4):
            for part in range(RINGP):
                for way in range(2):
                    if far < 4 or on_last(way, part):
                        ring(n, g, way, far, part, True).wait_recv()

    def compute(n, g):
        run = products(n, g, 0, 2, CHUNK, jnp.zeros((k, 128), F32))
        for part in range(2):
            for m in range(2):
                def other(c, a):
                    for b in range(8):
                        osend[n][g][c, b] = sums[g, index[2, c * 8 + b]].astype(osend[n][g].dtype)
                    return a

                first = m * 16 + 8 * (1 - part)
                lax.fori_loop(first, first + 8, other, 0)
                twin_copy(n, g, m, part).start()
        products(n, g, 2 * CHUNK, 1, slots - 2 * CHUNK, run)

    def exchange(n, g, t):
        top = 16 >> t

        def send(i, a):
            d = top - 1 - i
            for m in range(2):
                if n > 0 and not is_wide(n, t):
                    half_copy(n - 1, g, m, t, d).wait_send()
                for s in range(t):
                    half_copy(n, g, m, s, (8 >> s) + d).wait_recv()
                for b in range(8):
                    v = total_of(n, g, m, d, b, t)
                    if is_wide(n, t):
                        wsend[g, m, d, b] = v
                    else:
                        hsend[g][m, d, b] = v.astype(BF16)
                half_copy(n, g, m, t, d).start()
            return a

        if t < 2:
            for m in range(2):
                twin_copy(n, g, m, t).wait_recv()
            lax.fori_loop(0, 8 >> t, send, 0)
        else:
            for i in range(3):
                send(i, 0)

    def update(n, g):
        for m in range(2):
            for t, d in ((0, 8), (1, 4), (2, 3), (2, 2), (2, 1)):
                half_copy(n, g, m, t, d).wait_recv()
            for b in range(8 * m, 8 * m + 8):
                now = out[b, pl.ds(g * k, k), :]
                residual = rhs[b, pl.ds(g * k, k), :] - now - total_of(n, g, m, 0, b % 8, 2, True)
                put(n + 1, g, b, now + apply(residual, b))

    turn(0, 12)
    for move in moves:
        move.wait()
    for n in range(ITERS):
        if n > 0:
            exchange(n - 1, 1, 0)
        relay(n, 0)
        if n > 0:
            exchange(n - 1, 1, 1)
            exchange(n - 1, 1, 2)
        else:
            begin(1)
            turn(12, 12)
        gathered(n, 0)
        compute(n, 0)
        if n > 0:
            update(n - 1, 1)
        exchange(n, 0, 0)
        relay(n, 1)
        exchange(n, 0, 1)
        exchange(n, 0, 2)
        gathered(n, 1)
        compute(n, 1)
        if n < ITERS - 1:
            update(n, 0)
    exchange(ITERS - 1, 1, 0)
    update(ITERS - 1, 0)
    for t in range(1, 3):
        exchange(ITERS - 1, 1, t)
    update(ITERS - 1, 1)

    for n in range(ITERS):
        for g in range(GROUPS):
            for way in range(2):
                for far in range(1, 5):
                    for part in range(RINGP):
                        if far < 4 or on_last(way, part):
                            ring(n, g, way, far, part).wait_send()
            for m in range(2):
                for part in range(2):
                    twin_copy(n, g, m, part).wait_send()
                for t, places in enumerate((range(8, 16), range(4, 8), range(1, 4))):
                    for d in places:
                        if n == ITERS - 1 or is_wide(n + 1, t):
                            half_copy(n, g, m, t, d).wait_send()


def per_device(block_values, block_rows, block_cols, block_counts, precond, right_side):
    owned, wide, bs = right_side.shape[1:]
    slots = block_values.shape[2]
    k = wide // GROUPS
    vmem = pl.BlockSpec(memory_space=pltpu.VMEM)
    dma = pltpu.SemaphoreType.DMA
    result = pl.pallas_call(
        kernel,
        out_shape=jax.ShapeDtypeStruct((owned, wide, bs), F32),
        in_specs=[vmem, vmem, vmem, pl.BlockSpec(memory_space=pl.ANY), vmem, vmem],
        out_specs=vmem,
        scratch_shapes=[
            pltpu.VMEM((slots, bs, bs), BF16),
            pltpu.VMEM((slots, bs, bs), BF16),
            pltpu.VMEM((owned, bs, 2 * bs), BF16),
            pltpu.VMEM((GROUPS, slots + 1, k, bs), F32),
            pltpu.VMEM((CHUNK, k, bs), F32)]
        + [pltpu.VMEM((GROUPS, 2, 16 >> WIDE, 8, k, bs), F32)] * 2
        + [pltpu.VMEM((8, 512), jnp.int32), pltpu.VMEM((8, 512), F32),
           pltpu.SMEM((8, 512), jnp.int32), pltpu.SMEM((8, 512), F32)]
        + [pltpu.VMEM((8, owned, k, bs), BF16)] * (ITERS * GROUPS)
        + ([pltpu.VMEM((32, 8, k, bs), BF16)] * ((ITERS - 1) * GROUPS)
           + [pltpu.VMEM((32, 8, k, bs), F32)] * GROUPS) * 2
        + [pltpu.VMEM((2, 16, 8, k, bs), BF16)] * (GROUPS + ITERS * GROUPS)
        + [
            dma, dma, dma,
            dma((ITERS, GROUPS, 2, 4, RINGP)), dma((ITERS, GROUPS, 2, 4, RINGP)),
            dma((ITERS, GROUPS, 2, 2)), dma((ITERS, GROUPS, 2, 2)),
            dma((ITERS, GROUPS, 2, 16)), dma((ITERS, GROUPS, 2, 16)),
        ],
        compiler_params=pltpu.CompilerParams(
            collective_id=0, has_side_effects=True, vmem_limit_bytes=58 << 20),
    )(block_rows[0], block_cols[0], block_counts, block_values[0, 0], precond[0], right_side[0])
    return result[None]


def solution(mesh):
    placed = (
        P("row", "col", None, None, None),
        P("row", "col", None),
        P("row", "col", None),
        P("row", "col"),
        P("col", "row", None, None),
        P("col", "row", None, None),
    )
    return jax.shard_map(
        per_device,
        mesh=mesh,
        in_specs=placed,
        out_specs=P("col", "row", None, None),
        check_vma=False,
    )
```
